32 devices in a mesh: group: 2 (over y), tm: 8 (over z, core), pix: 2 (over x), sub: 1.
Axes of the slice: x: 2, y: 2, z: 4, core: 2. Of those that a mesh axis runs over, the one named last changes fastest.
Arguments:
- anomaly: bfloat16 [512, 65536], P('tm', ('group', 'pix', 'sub')), parts along dimension 1, may hold values from -6 to 6
- offsets: int32 [32], replicated, may hold values from 0 to 256, as said below
- taper_index: int32 [32], replicated, may hold values from 0 to 3
Outputs:
- spectral_gram: float32 [256, 64, 64], P(('group', 'tm')), parts along dimension 0
- leading_energy: float32 [256], P(('group', 'tm')), parts along dimension 0
The draws below stay inside these ranges and needn't reach their ends.
There are 2 independent parts, one for each index of `group`. The reference program is written for one: setup_inputs(seed, part) draws one part's arguments, and reference() takes and returns one part's arrays. A program takes and returns all parts, laid end to end along the dimension named above; an argument that names none is the same for every part. Nothing has to cross between parts.
Inputs may be any that keep to these rules, and one draw needn't show every extreme that they name: `offsets`: block starts never fall; the first block starts at day 0 and the last at day 512 - 256.
All inputs are finite; a program needn't handle non-finite values.
Results may differ from the reference program's by a relative error of at most 0.0034.
Values may be sent and summed in bfloat16 or wider, within the bound.
A program may use at most 128 MiB of HBM per device.

```python
import math
import jax
import jax.numpy as jnp
from jax import lax

NFFT = 256
NB = 32
POWER = 8
PIX_DEV = 16384
NF = 128
DAYS = 512
PIXELS = 32768


def draw_offsets(key, part):
    stride = (DAYS - NFFT) // (NB - 1)
    jitter = jax.random.randint(key, (NB,), 0, stride // 2 + 1)
    blocks = jnp.arange(NB, dtype=jnp.int32)
    starts = blocks * stride + jitter.astype(jnp.int32)
    starts = jnp.where(blocks == 0, 0, starts)
    starts = jnp.where(blocks == NB - 1, DAYS - NFFT, starts)
    return starts.astype(jnp.int32)


def set_ends(values, rng, smallest, top_value):
    dims = values.shape
    place = [jax.random.randint(jax.random.fold_in(rng, axis), (), 0, dims[axis]) for axis in range(len(dims))]
    values = values.at[tuple(place)].set(smallest)
    longest = dims.index(max(dims))
    place[longest] = (place[longest] + 1) % dims[longest]
    return values.at[tuple(place)].set(top_value)


def levels(key, extent, pieces, smallest, largest):
    def one(position, blocks):
        steps = jax.random.uniform(jax.random.fold_in(jax.random.fold_in(key, 6), position), (blocks,), jnp.float32, smallest / len(pieces), largest / len(pieces))
        return jnp.repeat(jnp.exp(steps), extent[position] // blocks).reshape((-1,) + (1,) * (len(extent) - position - 1))

    loudness = one(*pieces[0])
    for cut in pieces[1:]:
        loudness = loudness * one(*cut)
    return loudness


def scatter_about(rng, shape, scale, bound, pieces=(), kind=jnp.bfloat16):
    result = scale * jax.random.normal(rng, shape, jnp.float32)
    if pieces:
        result = result * levels(rng, shape, pieces, -0.22, 0.18)
    return jnp.clip(result, -bound, bound).astype(kind)


def setup_inputs(seed: int = 0, part: int = 0) -> dict:
    streams_of = jax.random.split(jax.random.key(seed), 4)
    part_keys = jax.random.split(jax.random.fold_in(streams_of[3], part), 4)
    anomaly = scatter_about(part_keys[0], (DAYS, PIXELS), 1.0, 6.0, ((0, 8), (1, 2)))
    offsets = draw_offsets(jax.random.fold_in(streams_of[3], 71), part)
    taper_index = set_ends(jax.random.randint(streams_of[2], (NB,), 0, 4), jax.random.fold_in(streams_of[2], 1), 0, 3).astype(jnp.int32)
    return dict(anomaly=anomaly, offsets=offsets, taper_index=taper_index)


power_eps = 1e-06

def window_rows(taper_index, length):
    steps_t = jnp.arange(length, dtype=jnp.float32)
    phase = steps_t * (2.0 * math.pi / length)
    center = (steps_t + 0.5) * (math.pi / length)
    hann = jnp.sin(center) ** 2
    hamming = 0.54 - 0.46 * jnp.cos(phase)
    blackman = 0.42 - 0.5 * jnp.cos(phase) + 0.08 * jnp.cos(2.0 * phase)
    sine_win = jnp.sin(center)
    table_rows = jnp.stack([hann, hamming, blackman, sine_win])
    chosen = jnp.zeros((taper_index.shape[0], length), jnp.float32)
    for which in range(4):
        chosen = chosen + jnp.where(taper_index[:, None] == which, table_rows[which][None, :], jnp.float32(0.0))
    return chosen

def dft_table(length, kept):
    freqs = jnp.arange(kept, dtype=jnp.int32)
    times = jnp.arange(length, dtype=jnp.int32)
    product = freqs[:, None] * times[None, :] % length
    angle = product.astype(jnp.float32) * (2.0 * math.pi / length)
    return jnp.stack([jnp.cos(angle), -jnp.sin(angle)]).astype(jnp.bfloat16)

def reference(anomaly, offsets, taper_index):
    windows = window_rows(taper_index, NFFT)
    energy = 1.0 / jnp.sqrt(lax.optimization_barrier(jnp.sum(windows * windows, axis=1)))
    transform = dft_table(NFFT, NF).astype(jnp.float32)
    spans = PIXELS // PIX_DEV

    def one_span(running, span_index):
        columns = lax.dynamic_slice_in_dim(anomaly, (span_index * PIX_DEV).astype(jnp.int32), PIX_DEV, 1)
        segments = jax.vmap(lambda first_day: lax.dynamic_slice_in_dim(columns, first_day.astype(jnp.int32), NFFT, 0))(offsets)
        windowed = (segments.astype(jnp.float32) * windows[:, :, None]).astype(jnp.bfloat16)
        spectra = jnp.einsum('rkt,btp->rbkp', transform, windowed.astype(jnp.float32))
        spectra = (spectra * energy[None, :, None, None]).astype(jnp.bfloat16)
        stacked = spectra.reshape(2 * NB, NF, PIX_DEV).astype(jnp.float32)
        return (running + jnp.einsum('ifp,jfp->fij', stacked, stacked), None)
    start_sum = jnp.zeros((NF, 2 * NB, 2 * NB), jnp.float32)
    summed, _ = lax.scan(one_span, start_sum, jnp.arange(spans, dtype=jnp.int32))
    spectral_gram = summed / PIXELS
    vector = jnp.ones((NF, 2 * NB), jnp.float32)
    for _ in range(POWER):
        applied = jnp.einsum('fij,fj->fi', spectral_gram, vector, precision=lax.Precision.HIGHEST)
        vector = applied / jnp.sqrt(lax.optimization_barrier(jnp.mean(applied * applied, axis=1, keepdims=True)) + power_eps)
    applied = jnp.einsum('fij,fj->fi', spectral_gram, vector, precision=lax.Precision.HIGHEST)
    leading_energy = jnp.sqrt(lax.optimization_barrier(jnp.mean(applied * applied, axis=1)))
    return (spectral_gram, leading_energy)
```

```python
import math

import jax
import jax.numpy as jnp
from jax import lax
from jax.sharding import PartitionSpec as P

NFFT = 256
NB = 32
POWER = 8
NF = 128


power_eps = 1e-06


def window_at(taper_index, steps_t, length):
    steps = steps_t.astype(jnp.float32)
    phase = steps * (2.0 * math.pi / length)
    center = (steps + 0.5) * (math.pi / length)
    hann = jnp.sin(center) ** 2
    hamming = 0.54 - 0.46 * jnp.cos(phase)
    blackman = 0.42 - 0.5 * jnp.cos(phase) + 0.08 * jnp.cos(2.0 * phase)
    sine_win = jnp.sin(center)
    which = taper_index[:, None]
    return jnp.where(
        which == 0, hann, jnp.where(which == 1, hamming, jnp.where(which == 2, blackman, sine_win))
    )


def day_operator(offsets, taper_index, freqs, days, length):
    day = jnp.arange(days, dtype=jnp.int32)
    step = day[None, :] - offsets[:, None]
    inside = (step >= 0) & (step < length)
    windows = jnp.where(inside, window_at(taper_index, step, length), 0.0)
    energy = 1.0 / jnp.sqrt(jnp.sum(windows * windows, axis=1, keepdims=True))
    scaled = windows * energy
    product = (freqs[:, None, None] * step[None]) & (length - 1)
    angle = product.astype(jnp.float32) * (2.0 * math.pi / length)
    table = jnp.stack([jnp.cos(angle), -jnp.sin(angle)], axis=1)
    table = lax.reduce_precision(table, 8, 7)
    return (table * scaled).reshape(freqs.shape[0], 2 * offsets.shape[0], days)


def shards(anomaly, offsets, taper_index):
    series = lax.all_to_all(anomaly, "tm", split_axis=1, concat_axis=0, tiled=True)
    days = series.shape[0]
    own = NF // lax.axis_size("tm")
    freqs = lax.axis_index("tm") * own + jnp.arange(own, dtype=jnp.int32)
    operator = day_operator(offsets, taper_index, freqs, days, NFFT)
    covariance = jnp.einsum("dp,ep->de", series, series, preferred_element_type=jnp.float32)
    covariance = lax.psum(covariance, ("tm", "pix", "sub"))
    total_pixels = anomaly.shape[1] * lax.axis_size(("pix", "sub"))
    half = jnp.einsum("fid,de->fie", operator, covariance, precision=lax.Precision.HIGH)
    spectral_gram = jnp.einsum("fie,fje->fij", half, operator, precision=lax.Precision.HIGH)
    spectral_gram = spectral_gram / total_pixels
    vector = jnp.ones((own, 2 * NB), jnp.float32)
    for _ in range(POWER):
        applied = jnp.einsum("fij,fj->fi", spectral_gram, vector, precision=lax.Precision.HIGHEST)
        vector = applied / jnp.sqrt(jnp.mean(applied * applied, axis=1, keepdims=True) + power_eps)
    applied = jnp.einsum("fij,fj->fi", spectral_gram, vector, precision=lax.Precision.HIGHEST)
    leading_energy = jnp.sqrt(jnp.mean(applied * applied, axis=1))
    return (spectral_gram, leading_energy)


def solution(mesh):
    placed = (P("tm", ("group", "pix", "sub")), P(), P())
    return jax.shard_map(
        shards,
        mesh=mesh,
        in_specs=placed,
        out_specs=(P(("group", "tm"), None, None), P(("group", "tm"))),
        check_vma=False,
    )
```

```python
import functools
import math

import jax
import jax.numpy as jnp
from jax import lax
from jax.experimental import pallas as pl
from jax.experimental.pallas import tpu as pltpu
from jax.sharding import PartitionSpec as P

NFFT = 256
NB = 32
POWER = 8
NF = 128


power_eps = 1e-06


def window_at(taper_index, steps_t, length):
    steps = steps_t.astype(jnp.float32)
    phase = steps * (2.0 * math.pi / length)
    center = (steps + 0.5) * (math.pi / length)
    hann = jnp.sin(center) ** 2
    hamming = 0.54 - 0.46 * jnp.cos(phase)
    blackman = 0.42 - 0.5 * jnp.cos(phase) + 0.08 * jnp.cos(2.0 * phase)
    sine_win = jnp.sin(center)
    which = taper_index[:, None]
    return jnp.where(
        which == 0, hann, jnp.where(which == 1, hamming, jnp.where(which == 2, blackman, sine_win))
    )


def day_operator(offsets, taper_index, freqs, days, length):
    day = jnp.arange(days, dtype=jnp.int32)
    step = day[None, :] - offsets[:, None]
    inside = (step >= 0) & (step < length)
    windows = jnp.where(inside, window_at(taper_index, step, length), 0.0)
    energy = 1.0 / jnp.sqrt(jnp.sum(windows * windows, axis=1, keepdims=True))
    scaled = windows * energy
    product = (freqs[:, None, None] * step[None]) & (length - 1)
    angle = product.astype(jnp.float32) * (2.0 * math.pi / length)
    table = jnp.stack([jnp.cos(angle), -jnp.sin(angle)], axis=1)
    table = lax.reduce_precision(table, 8, 7)
    return (table * scaled).reshape(freqs.shape[0], 2 * offsets.shape[0], days)


BLOCK = 128
MESH = pl.DeviceIdType.MESH


def stages_of(tm, pix, sub):
    if sub > 1 or tm % 2:
        split = [("sub", 1, sub), ("pix", 1, pix), ("tm", 1, tm)]
    else:
        split = [("tm", 1, 2), ("pix", 1, pix), ("tm", 2, tm // 2)]
    return [stage for stage in split if stage[2] > 1]


def place_in(stage):
    axis, inner, members = stage
    return lax.rem(lax.axis_index(axis) // inner, members)


def device_at(stage, shift):
    axis, inner, members = stage
    index = lax.axis_index(axis)
    here = place_in(stage)
    there = lax.rem(here + shift, members)
    return {axis: index + (there - here) * inner}, there


def covariance_kernel(stages, series, out, packed, gathered, *scratch):
    count = len(stages)
    landing = scratch[:count]
    sems = scratch[count:]
    days = series.shape[0]
    blocks = days // BLOCK

    barrier = pltpu.get_barrier_semaphore()
    for stage in stages:
        for shift in range(1, stage[2]):
            pl.semaphore_signal(barrier, inc=1, device_id=device_at(stage, shift)[0], device_id_type=MESH)

    place = 0
    for i in range(blocks):
        strip = lax.dot_general(
            series[i * BLOCK : (i + 1) * BLOCK, :],
            series[i * BLOCK :, :],
            (((1,), (1,)), ((), ())),
            preferred_element_type=jnp.float32,
        )
        for j in range(blocks - i):
            packed[pl.ds((place + j) * BLOCK, BLOCK), :] = strip[:, j * BLOCK : (j + 1) * BLOCK]
        place += blocks - i
    if packed.shape[0] > place * BLOCK:
        packed[place * BLOCK :, :] = jnp.zeros((packed.shape[0] - place * BLOCK, BLOCK), jnp.float32)
    pl.semaphore_wait(barrier, sum(stage[2] - 1 for stage in stages))

    start, rows = 0, packed.shape[0]
    starts = []
    for s, stage in enumerate(stages):
        members = stage[2]
        part = rows // members
        starts.append(start)
        copies = []
        for shift in range(1, members):
            device, there = device_at(stage, shift)
            copy = pltpu.make_async_remote_copy(
                src_ref=packed.at[pl.ds(pl.multiple_of(start + there * part, 8), part), :],
                dst_ref=landing[s].at[shift - 1],
                send_sem=sems[4 * s].at[shift - 1],
                recv_sem=sems[4 * s + 1].at[shift - 1],
                device_id=device,
                device_id_type=MESH,
            )
            copy.start()
            copies.append(copy)
        start = start + place_in(stage) * part
        rows = part
        own = packed.at[pl.ds(pl.multiple_of(start, 8), part), :]
        total = own[...]
        for shift in range(1, members):
            copies[shift - 1].wait()
            total = total + landing[s][shift - 1]
        own[...] = total
    gathered[pl.ds(pl.multiple_of(start, 8), rows), :] = total

    for s in reversed(range(count)):
        stage = stages[s]
        own = gathered.at[pl.ds(pl.multiple_of(start, 8), rows), :]
        copies = []
        for shift in range(1, stage[2]):
            copy = pltpu.make_async_remote_copy(
                src_ref=own,
                dst_ref=own,
                send_sem=sems[4 * s + 2].at[shift - 1],
                recv_sem=sems[4 * s + 3].at[shift - 1],
                device_id=device_at(stage, shift)[0],
                device_id_type=MESH,
            )
            copy.start()
            copies.append(copy)
        for copy in copies:
            copy.wait()
        start, rows = starts[s], rows * stage[2]

    place = 0
    for i in range(blocks):
        for j in range(i, blocks):
            block = gathered[pl.ds(place * BLOCK, BLOCK), :]
            out[pl.ds(i * BLOCK, BLOCK), pl.ds(j * BLOCK, BLOCK)] = block
            if j > i:
                out[pl.ds(j * BLOCK, BLOCK), pl.ds(i * BLOCK, BLOCK)] = block.T
            place += 1


def summed_covariance(series):
    days = series.shape[0]
    stages = stages_of(lax.axis_size("tm"), lax.axis_size("pix"), lax.axis_size("sub"))
    devices = math.prod(stage[2] for stage in stages)
    blocks = days // BLOCK
    rows = -(-(blocks * (blocks + 1) // 2 * BLOCK) // (8 * devices)) * 8 * devices
    landing, sems, part = [], [], rows
    for stage in stages:
        part //= stage[2]
        landing.append(pltpu.VMEM((stage[2] - 1, part, BLOCK), jnp.float32))
        sems += [pltpu.SemaphoreType.DMA((stage[2] - 1,))] * 4
    return pl.pallas_call(
        functools.partial(covariance_kernel, stages),
        out_shape=jax.ShapeDtypeStruct((days, days), jnp.float32),
        in_specs=[pl.BlockSpec(memory_space=pltpu.VMEM)],
        out_specs=pl.BlockSpec(memory_space=pltpu.VMEM),
        scratch_shapes=[pltpu.VMEM((rows, BLOCK), jnp.float32)] * 2 + landing + sems,
        compiler_params=pltpu.CompilerParams(
            collective_id=0, has_side_effects=True, vmem_limit_bytes=48 * 2**20
        ),
        name="covariance",
    )(series)


def leading_kernel(gram_ref, lead_ref):
    gram = gram_ref[...]
    size = gram.shape[1]
    vector = jnp.ones((gram.shape[0], 1, size), jnp.float32)
    for step in range(POWER + 1):
        across = 2 - step % 2
        applied = jnp.sum(gram * vector, axis=across, keepdims=True)
        power = jnp.sum(applied * applied, axis=3 - across, keepdims=True) / size
        vector = applied / jnp.sqrt(power + power_eps)
    lead_ref[...] = jnp.broadcast_to(jnp.sqrt(power)[:, 0, :], lead_ref.shape)


def leading_mode(spectral_gram):
    own = spectral_gram.shape[0]
    lead = pl.pallas_call(
        leading_kernel,
        out_shape=jax.ShapeDtypeStruct((own, BLOCK), jnp.float32),
        in_specs=[pl.BlockSpec(memory_space=pltpu.VMEM)],
        out_specs=pl.BlockSpec(memory_space=pltpu.VMEM),
        name="leading",
    )(spectral_gram)
    return lead[:, 0]


def shards(anomaly, offsets, taper_index):
    series = lax.all_to_all(anomaly, "tm", split_axis=1, concat_axis=0, tiled=True)
    own = NF // lax.axis_size("tm")
    freqs = lax.axis_index("tm") * own + jnp.arange(own, dtype=jnp.int32)
    total_pixels = anomaly.shape[1] * lax.axis_size(("pix", "sub"))
    operator = day_operator(offsets, taper_index, freqs, series.shape[0], NFFT)
    covariance = summed_covariance(series)
    half = jnp.einsum("fid,de->fie", operator, covariance, precision=lax.Precision.HIGH)
    spectral_gram = jnp.einsum("fie,fje->fij", half, operator, precision=lax.Precision.HIGH)
    spectral_gram = spectral_gram / total_pixels
    return (spectral_gram, leading_mode(spectral_gram))


def solution(mesh):
    placed = (P("tm", ("group", "pix", "sub")), P(), P())
    return jax.shard_map(
        shards,
        mesh=mesh,
        in_specs=placed,
        out_specs=(P(("group", "tm"), None, None), P(("group", "tm"))),
        check_vma=False,
    )
```

```python
import functools
import math

import jax
import jax.numpy as jnp
from jax import lax
from jax.experimental import pallas as pl
from jax.experimental.pallas import tpu as pltpu
from jax.sharding import PartitionSpec as P

NFFT = 256
NB = 32
POWER = 8
NF = 128


power_eps = 1e-06


CHUNKS = 4


def windows_of(taper, step, length):
    steps = step.astype(jnp.float32)
    phase = steps * (2.0 * math.pi / length)
    center = (steps + 0.5) * (math.pi / length)
    sine_win = jnp.sin(center)
    hann = sine_win * sine_win
    hamming = 0.54 - 0.46 * jnp.cos(phase)
    blackman = 0.42 - 0.5 * jnp.cos(phase) + 0.08 * jnp.cos(2.0 * phase)
    chosen = jnp.where(
        taper == 0, hann, jnp.where(taper == 1, hamming, jnp.where(taper == 2, blackman, sine_win))
    )
    return jnp.where((step >= 0) & (step < length), chosen, 0.0)


def write_operator(offsets, taper, operator):
    own, _, days = operator.shape
    step = lax.broadcasted_iota(jnp.int32, (NB, days), 1) - offsets[...]
    windows = windows_of(jnp.broadcast_to(taper[...], (NB, days)), step, NFFT)
    scaled = windows * (1.0 / jnp.sqrt(jnp.sum(windows * windows, axis=1, keepdims=True)))
    first = lax.axis_index("tm") * own

    def one(f, carry):
        angle = (((first + f) * step) & (NFFT - 1)).astype(jnp.float32) * (2.0 * math.pi / NFFT)
        operator[f, :NB, :] = jnp.cos(angle).astype(jnp.bfloat16).astype(jnp.float32) * scaled
        operator[f, NB:, :] = (-jnp.sin(angle)).astype(jnp.bfloat16).astype(jnp.float32) * scaled
        return carry

    lax.fori_loop(0, own, one, 0)


BLOCK = 128
MESH = pl.DeviceIdType.MESH


def stages_of(tm, pix, sub):
    if sub > 1 or tm % 2:
        split = [("sub", 1, sub), ("pix", 1, pix), ("tm", 1, tm)]
    else:
        split = [("tm", 1, 2), ("pix", 1, pix), ("tm", 2, tm // 2)]
    return [stage for stage in split if stage[2] > 1]


def place_in(stage):
    axis, inner, members = stage
    return lax.rem(lax.axis_index(axis) // inner, members)


def device_at(stage, shift):
    axis, inner, members = stage
    index = lax.axis_index(axis)
    here = place_in(stage)
    there = lax.rem(here + shift, members)
    return {axis: index + (there - here) * inner}, there


def add_products(series, packed, first):
    blocks = series.shape[0] // BLOCK
    place = 0
    for i in range(blocks):
        strip = lax.dot_general(
            series[i * BLOCK : (i + 1) * BLOCK, :],
            series[i * BLOCK :, :],
            (((1,), (1,)), ((), ())),
            preferred_element_type=jnp.float32,
        )
        for j in range(blocks - i):
            rows = pl.ds((place + j) * BLOCK, BLOCK)
            block = strip[:, j * BLOCK : (j + 1) * BLOCK]
            packed[rows, :] = block if first else packed[rows, :] + block
        place += blocks - i


def covariance_kernel(
    stages, anomaly, offsets, taper, out, operator, series, packed, gathered, own_sem, *scratch
):
    exchange_send, exchange_recv = scratch[:2]
    count = len(stages)
    landing = scratch[2 : 2 + count]
    sems = scratch[2 + count :]
    chunks, days, width = series.shape
    per_device = anomaly.shape[0]
    peers = days // per_device
    me = lax.axis_index("tm")

    barrier = pltpu.get_barrier_semaphore()
    greeted = 0
    for axis in ("tm", "pix", "sub"):
        members = lax.axis_size(axis)
        for shift in range(1, members):
            device = {axis: lax.rem(lax.axis_index(axis) + shift, members)}
            pl.semaphore_signal(barrier, inc=1, device_id=device, device_id_type=MESH)
            greeted += 1
    my_rows = pl.ds(pl.multiple_of(me * per_device, per_device), per_device)

    def columns(device, chunk):
        return pl.ds(pl.multiple_of(device * (chunks * width) + chunk * width, width), width)

    kept = []
    for chunk in range(chunks):
        copy = pltpu.make_async_copy(
            anomaly.at[:, columns(me, chunk)], series.at[chunk, my_rows, :], own_sem.at[chunk]
        )
        copy.start()
        kept.append(copy)
    pl.semaphore_wait(barrier, greeted)
    farthest_first = sorted(range(1, peers), key=lambda shift: abs(2 * shift - peers))
    exchanged = []
    for chunk in range(chunks):
        copies = []
        for shift in farthest_first:
            there = lax.rem(me + shift, peers)
            copy = pltpu.make_async_remote_copy(
                src_ref=anomaly.at[:, columns(there, chunk)],
                dst_ref=series.at[chunk, my_rows, :],
                send_sem=exchange_send.at[chunk, shift - 1],
                recv_sem=exchange_recv.at[chunk, shift - 1],
                device_id={"tm": there},
                device_id_type=MESH,
            )
            copy.start()
            copies.append(copy)
        exchanged.append(copies)

    write_operator(offsets, taper, operator)
    blocks = days // BLOCK
    filled = blocks * (blocks + 1) // 2 * BLOCK
    if packed.shape[0] > filled:
        packed[filled:, :] = jnp.zeros((packed.shape[0] - filled, BLOCK), jnp.float32)
    for chunk in range(chunks):
        kept[chunk].wait()
        for copy in exchanged[chunk]:
            copy.wait()
        add_products(series.at[chunk], packed, chunk == 0)

    start, rows = 0, packed.shape[0]
    starts = []
    for s, stage in enumerate(stages):
        members = stage[2]
        part = rows // members
        starts.append(start)
        copies = []
        for shift in range(1, members):
            device, there = device_at(stage, shift)
            copy = pltpu.make_async_remote_copy(
                src_ref=packed.at[pl.ds(pl.multiple_of(start + there * part, 8), part), :],
                dst_ref=landing[s].at[shift - 1],
                send_sem=sems[4 * s].at[shift - 1],
                recv_sem=sems[4 * s + 1].at[shift - 1],
                device_id=device,
                device_id_type=MESH,
            )
            copy.start()
            copies.append(copy)
        start = start + place_in(stage) * part
        rows = part
        own = packed.at[pl.ds(pl.multiple_of(start, 8), part), :]
        total = own[...]
        for shift in range(1, members):
            copies[shift - 1].wait()
            total = total + landing[s][shift - 1]
        own[...] = total
    gathered[pl.ds(pl.multiple_of(start, 8), rows), :] = total

    for s in reversed(range(count)):
        stage = stages[s]
        own = gathered.at[pl.ds(pl.multiple_of(start, 8), rows), :]
        copies = []
        for shift in range(1, stage[2]):
            copy = pltpu.make_async_remote_copy(
                src_ref=own,
                dst_ref=own,
                send_sem=sems[4 * s + 2].at[shift - 1],
                recv_sem=sems[4 * s + 3].at[shift - 1],
                device_id=device_at(stage, shift)[0],
                device_id_type=MESH,
            )
            copy.start()
            copies.append(copy)
        for copy in copies:
            copy.wait()
        start, rows = starts[s], rows * stage[2]

    place = 0
    for i in range(blocks):
        for j in range(i, blocks):
            block = gathered[pl.ds(place * BLOCK, BLOCK), :]
            out[pl.ds(i * BLOCK, BLOCK), pl.ds(j * BLOCK, BLOCK)] = block
            if j > i:
                out[pl.ds(j * BLOCK, BLOCK), pl.ds(i * BLOCK, BLOCK)] = block.T
            place += 1


def covariance_and_operator(anomaly, offsets, taper_index):
    per_device, pixels = anomaly.shape
    peers = lax.axis_size("tm")
    days = per_device * peers
    own = NF // peers
    stages = stages_of(peers, lax.axis_size("pix"), lax.axis_size("sub"))
    devices = math.prod(stage[2] for stage in stages)
    blocks = days // BLOCK
    rows = -(-(blocks * (blocks + 1) // 2 * BLOCK) // (8 * devices)) * 8 * devices
    landing, sems, part = [], [], rows
    for stage in stages:
        part //= stage[2]
        landing.append(pltpu.VMEM((stage[2] - 1, part, BLOCK), jnp.float32))
        sems += [pltpu.SemaphoreType.DMA((stage[2] - 1,))] * 4
    vmem = pl.BlockSpec(memory_space=pltpu.VMEM)
    return pl.pallas_call(
        functools.partial(covariance_kernel, stages),
        out_shape=(
            jax.ShapeDtypeStruct((days, days), jnp.float32),
            jax.ShapeDtypeStruct((own, 2 * NB, days), jnp.float32),
        ),
        in_specs=[pl.BlockSpec(memory_space=pl.ANY), vmem, vmem],
        out_specs=(vmem, vmem),
        scratch_shapes=[
            pltpu.VMEM((CHUNKS, days, pixels // peers // CHUNKS), jnp.bfloat16),
            pltpu.VMEM((rows, BLOCK), jnp.float32),
            pltpu.VMEM((rows, BLOCK), jnp.float32),
            pltpu.SemaphoreType.DMA((CHUNKS,)),
            pltpu.SemaphoreType.DMA((CHUNKS, peers - 1)),
            pltpu.SemaphoreType.DMA((CHUNKS, peers - 1)),
        ]
        + landing
        + sems,
        compiler_params=pltpu.CompilerParams(
            collective_id=0, has_side_effects=True, vmem_limit_bytes=56 * 2**20
        ),
        name="covariance",
    )(anomaly, offsets[:, None], taper_index[:, None])


def leading_kernel(gram_ref, lead_ref):
    gram = gram_ref[...]
    size = gram.shape[1]
    vector = jnp.ones((gram.shape[0], 1, size), jnp.float32)
    for step in range(POWER + 1):
        across = 2 - step % 2
        applied = jnp.sum(gram * vector, axis=across, keepdims=True)
        power = jnp.sum(applied * applied, axis=3 - across, keepdims=True) / size
        vector = applied / jnp.sqrt(power + power_eps)
    lead_ref[...] = jnp.broadcast_to(jnp.sqrt(power)[:, 0, :], lead_ref.shape)


def leading_mode(spectral_gram):
    own = spectral_gram.shape[0]
    lead = pl.pallas_call(
        leading_kernel,
        out_shape=jax.ShapeDtypeStruct((own, BLOCK), jnp.float32),
        in_specs=[pl.BlockSpec(memory_space=pltpu.VMEM)],
        out_specs=pl.BlockSpec(memory_space=pltpu.VMEM),
        name="leading",
    )(spectral_gram)
    return lead[:, 0]


def shards(anomaly, offsets, taper_index):
    total_pixels = anomaly.shape[1] * lax.axis_size(("pix", "sub"))
    covariance, operator = covariance_and_operator(anomaly, offsets, taper_index)
    half = jnp.einsum("fid,de->fie", operator, covariance, precision=lax.Precision.HIGH)
    spectral_gram = jnp.einsum("fie,fje->fij", half, operator, precision=lax.Precision.HIGH)
    spectral_gram = spectral_gram / total_pixels
    return (spectral_gram, leading_mode(spectral_gram))


def solution(mesh):
    placed = (P("tm", ("group", "pix", "sub")), P(), P())
    return jax.shard_map(
        shards,
        mesh=mesh,
        in_specs=placed,
        out_specs=(P(("group", "tm"), None, None), P(("group", "tm"))),
        check_vma=False,
    )
```

```python
import functools
import math

import jax
import jax.numpy as jnp
from jax import lax
from jax.experimental import pallas as pl
from jax.experimental.pallas import tpu as pltpu
from jax.sharding import PartitionSpec as P

NFFT = 256
NB = 32
POWER = 8
NF = 128


power_eps = 1e-06


CHUNKS = 4


def windows_of(taper, step, length):
    steps = step.astype(jnp.float32)
    phase = steps * (2.0 * math.pi / length)
    center = (steps + 0.5) * (math.pi / length)
    sine_win = jnp.sin(center)
    hann = sine_win * sine_win
    hamming = 0.54 - 0.46 * jnp.cos(phase)
    blackman = 0.42 - 0.5 * jnp.cos(phase) + 0.08 * jnp.cos(2.0 * phase)
    chosen = jnp.where(
        taper == 0, hann, jnp.where(taper == 1, hamming, jnp.where(taper == 2, blackman, sine_win))
    )
    return jnp.where((step >= 0) & (step < length), chosen, 0.0)


def upright(row):
    square = (NB, NB)
    diagonal = lax.broadcasted_iota(jnp.int32, square, 0) == lax.broadcasted_iota(jnp.int32, square, 1)
    values = jnp.broadcast_to(row[...].astype(jnp.float32), square)
    return jnp.sum(jnp.where(diagonal, values, 0.0), axis=1, keepdims=True).astype(jnp.int32)


def write_operator(offsets, taper, operator):
    own, _, days = operator.shape
    step = lax.broadcasted_iota(jnp.int32, (NB, days), 1) - upright(offsets)
    windows = windows_of(jnp.broadcast_to(upright(taper), (NB, days)), step, NFFT)
    scaled = windows * (1.0 / jnp.sqrt(jnp.sum(windows * windows, axis=1, keepdims=True)))
    first = lax.axis_index("tm") * own

    def one(f, carry):
        angle = (((first + f) * step) & (NFFT - 1)).astype(jnp.float32) * (2.0 * math.pi / NFFT)
        operator[f, :NB, :] = jnp.cos(angle).astype(jnp.bfloat16).astype(jnp.float32) * scaled
        operator[f, NB:, :] = (-jnp.sin(angle)).astype(jnp.bfloat16).astype(jnp.float32) * scaled
        return carry

    lax.fori_loop(0, own, one, 0)


BLOCK = 128
MESH = pl.DeviceIdType.MESH


def stages_of(tm, pix, sub):
    if sub > 1 or tm % 2:
        split = [("sub", 1, sub), ("pix", 1, pix), ("tm", 1, tm)]
    else:
        split = [("tm", 1, 2), ("pix", 1, pix), ("tm", 2, tm // 2)]
    return split


def place_in(stage):
    axis, inner, members = stage
    return lax.rem(lax.axis_index(axis) // inner, members)


def device_at(stage, shift):
    axis, inner, members = stage
    index = lax.axis_index(axis)
    here = place_in(stage)
    there = lax.rem(here + shift, members)
    return {axis: index + (there - here) * inner}, there


def add_products(series, packed, first):
    blocks = series.shape[0] // BLOCK
    place = 0
    for i in range(blocks):
        strip = lax.dot_general(
            series[i * BLOCK : (i + 1) * BLOCK, :],
            series[i * BLOCK :, :],
            (((1,), (1,)), ((), ())),
            preferred_element_type=jnp.float32,
        )
        for j in range(blocks - i):
            rows = pl.ds((place + j) * BLOCK, BLOCK)
            block = strip[:, j * BLOCK : (j + 1) * BLOCK]
            packed[rows, :] = block if first else packed[rows, :] + block
        place += blocks - i


def covariance_kernel(
    stages, anomaly, offsets, taper, out, operator, series, packed, gathered, own_sem, *scratch
):
    exchange_send, exchange_recv = scratch[:2]
    landing, sems = scratch[2:5], scratch[5:]
    chunks, days, width = series.shape
    per_device = anomaly.shape[0]
    peers = days // per_device
    me = lax.axis_index("tm")

    barrier = pltpu.get_barrier_semaphore()
    greeted = 0
    for axis in ("tm", "pix", "sub"):
        members = lax.axis_size(axis)
        for shift in range(1, members):
            device = {axis: lax.rem(lax.axis_index(axis) + shift, members)}
            pl.semaphore_signal(barrier, inc=1, device_id=device, device_id_type=MESH)
            greeted += 1
    my_rows = pl.ds(pl.multiple_of(me * per_device, per_device), per_device)

    def columns(device, chunk):
        return pl.ds(pl.multiple_of(device * (chunks * width) + chunk * width, width), width)

    kept = []
    for chunk in range(chunks):
        copy = pltpu.make_async_copy(
            anomaly.at[:, columns(me, chunk)], series.at[chunk, my_rows, :], own_sem.at[chunk]
        )
        copy.start()
        kept.append(copy)
    pl.semaphore_wait(barrier, greeted)
    farthest_first = sorted(range(1, peers), key=lambda shift: abs(2 * shift - peers))
    exchanged = []
    for chunk in range(chunks):
        copies = []
        for shift in farthest_first:
            there = lax.rem(me + shift, peers)
            copy = pltpu.make_async_remote_copy(
                src_ref=anomaly.at[:, columns(there, chunk)],
                dst_ref=series.at[chunk, my_rows, :],
                send_sem=exchange_send.at[chunk, shift - 1],
                recv_sem=exchange_recv.at[chunk, shift - 1],
                device_id={"tm": there},
                device_id_type=MESH,
            )
            copy.start()
            copies.append(copy)
        exchanged.append(copies)

    write_operator(offsets, taper, operator)
    blocks = days // BLOCK
    filled = blocks * (blocks + 1) // 2 * BLOCK
    if packed.shape[0] > filled:
        packed[filled:, :] = jnp.zeros((packed.shape[0] - filled, BLOCK), jnp.float32)
    for chunk in range(chunks):
        kept[chunk].wait()
        for copy in exchanged[chunk]:
            copy.wait()
        add_products(series.at[chunk], packed, chunk == 0)

    near, side, line = stages
    piece = packed.shape[0] // line[2]
    half = piece // near[2]
    part = half // side[2]

    def rows_of(at, n, s, rows):
        return pl.ds(pl.multiple_of(at * piece + n * half + s * part, 8), rows)

    def send(src, dst, sem, index, device):
        copy = pltpu.make_async_remote_copy(
            src_ref=src,
            dst_ref=dst,
            send_sem=sems[2 * sem].at[index],
            recv_sem=sems[2 * sem + 1].at[index],
            device_id=device,
            device_id_type=MESH,
        )
        copy.start()
        return copy

    my_near, my_side = place_in(near), place_in(side)
    order = list(range(1, line[2])) + [0]
    order.sort(key=lambda shift: abs(2 * shift - line[2]))
    targets = {shift: device_at(line, shift) for shift in order}

    near_copies, side_copies, line_copies = {}, {}, {}
    for shift in order:
        at = targets[shift][1]
        near_copies[shift] = []
        for k in range(1, near[2]):
            device, there = device_at(near, k)
            index = shift * (near[2] - 1) + k - 1
            src = packed.at[rows_of(at, there, 0, half), :]
            near_copies[shift].append(send(src, landing[0].at[index], 0, index, device))
    for shift in order:
        at = targets[shift][1]
        mine = packed.at[rows_of(at, my_near, 0, half), :]
        total = mine[...]
        for k, copy in enumerate(near_copies[shift]):
            copy.wait()
            total = total + landing[0][shift * (near[2] - 1) + k]
        mine[...] = total
        side_copies[shift] = []
        for k in range(1, side[2]):
            device, there = device_at(side, k)
            index = shift * (side[2] - 1) + k - 1
            src = packed.at[rows_of(at, my_near, there, part), :]
            side_copies[shift].append(send(src, landing[1].at[index], 1, index, device))
    for shift in order:
        device, at = targets[shift]
        mine = packed.at[rows_of(at, my_near, my_side, part), :]
        total = mine[...]
        for k, copy in enumerate(side_copies[shift]):
            copy.wait()
            total = total + landing[1][shift * (side[2] - 1) + k]
        mine[...] = total
        if shift:
            line_copies[shift] = send(mine, landing[2].at[shift - 1], 2, shift - 1, device)
    here = place_in(line)
    own = gathered.at[rows_of(here, my_near, my_side, part), :]
    total = packed[rows_of(here, my_near, my_side, part), :]
    for shift in order:
        if shift:
            line_copies[shift].wait()
            total = total + landing[2][shift - 1]
    own[...] = total

    arriving = {}
    for shift in order:
        if shift:
            arriving[shift] = send(own, own, 3, shift - 1, targets[shift][0])
    spread, near_spread = {}, []
    incoming = [0] + [shift for shift in order if shift]
    sources = {shift: lax.rem(here + line[2] - shift, line[2]) for shift in incoming}
    for shift in incoming:
        if shift:
            arriving[shift].wait()
        mine = gathered.at[rows_of(sources[shift], my_near, my_side, part), :]
        spread[shift] = [
            send(mine, mine, 4, shift * (side[2] - 1) + k - 1, device_at(side, k)[0])
            for k in range(1, side[2])
        ]
    for shift in incoming:
        for copy in spread[shift]:
            copy.wait()
        mine = gathered.at[rows_of(sources[shift], my_near, 0, half), :]
        near_spread += [
            send(mine, mine, 5, shift * (near[2] - 1) + k - 1, device_at(near, k)[0])
            for k in range(1, near[2])
        ]
    for copy in near_spread:
        copy.wait()

    place = 0
    for i in range(blocks):
        for j in range(i, blocks):
            block = gathered[pl.ds(place * BLOCK, BLOCK), :]
            out[pl.ds(i * BLOCK, BLOCK), pl.ds(j * BLOCK, BLOCK)] = block
            if j > i:
                out[pl.ds(j * BLOCK, BLOCK), pl.ds(i * BLOCK, BLOCK)] = block.T
            place += 1


def covariance_and_operator(anomaly, offsets, taper_index):
    per_device, pixels = anomaly.shape
    peers = lax.axis_size("tm")
    days = per_device * peers
    own = NF // peers
    stages = stages_of(peers, lax.axis_size("pix"), lax.axis_size("sub"))
    devices = math.prod(stage[2] for stage in stages)
    blocks = days // BLOCK
    rows = -(-(blocks * (blocks + 1) // 2 * BLOCK) // (8 * devices)) * 8 * devices
    near, side, line = (stage[2] for stage in stages)
    half = rows // line // near
    part = half // side
    slots = [max(1, count) for count in (line * (near - 1), line * (side - 1), line - 1)]
    landing = [
        pltpu.VMEM((count, depth, BLOCK), jnp.float32)
        for count, depth in zip(slots, (half, part, part))
    ]
    sems = [
        pltpu.SemaphoreType.DMA((slots[stage],)) for stage in (0, 1, 2, 2, 1, 0) for _ in range(2)
    ]
    vmem = pl.BlockSpec(memory_space=pltpu.VMEM)
    return pl.pallas_call(
        functools.partial(covariance_kernel, stages),
        out_shape=(
            jax.ShapeDtypeStruct((days, days), jnp.float32),
            jax.ShapeDtypeStruct((own, 2 * NB, days), jnp.float32),
        ),
        in_specs=[pl.BlockSpec(memory_space=pl.ANY), vmem, vmem],
        out_specs=(vmem, vmem),
        scratch_shapes=[
            pltpu.VMEM((CHUNKS, days, pixels // peers // CHUNKS), jnp.bfloat16),
            pltpu.VMEM((rows, BLOCK), jnp.float32),
            pltpu.VMEM((rows, BLOCK), jnp.float32),
            pltpu.SemaphoreType.DMA((CHUNKS,)),
            pltpu.SemaphoreType.DMA((CHUNKS, peers - 1)),
            pltpu.SemaphoreType.DMA((CHUNKS, peers - 1)),
        ]
        + landing
        + sems,
        compiler_params=pltpu.CompilerParams(
            collective_id=0, has_side_effects=True, vmem_limit_bytes=56 * 2**20
        ),
        name="covariance",
    )(anomaly, offsets[None, :], taper_index[None, :])


def leading_kernel(gram_ref, lead_ref):
    gram = gram_ref[...]
    size = gram.shape[1]
    vector = jnp.ones((gram.shape[0], 1, size), jnp.float32)
    for step in range(POWER + 1):
        across = 2 - step % 2
        applied = jnp.sum(gram * vector, axis=across, keepdims=True)
        power = jnp.sum(applied * applied, axis=3 - across, keepdims=True) / size
        vector = applied / jnp.sqrt(power + power_eps)
    lead_ref[...] = jnp.broadcast_to(jnp.sqrt(power)[:, 0, :], lead_ref.shape)


def leading_mode(spectral_gram):
    own = spectral_gram.shape[0]
    lead = pl.pallas_call(
        leading_kernel,
        out_shape=jax.ShapeDtypeStruct((own, BLOCK), jnp.float32),
        in_specs=[pl.BlockSpec(memory_space=pltpu.VMEM)],
        out_specs=pl.BlockSpec(memory_space=pltpu.VMEM),
        name="leading",
    )(spectral_gram)
    return lead[:, 0]


def shards(anomaly, offsets, taper_index):
    total_pixels = anomaly.shape[1] * lax.axis_size(("pix", "sub"))
    covariance, operator = covariance_and_operator(anomaly, offsets, taper_index)
    half = jnp.einsum("fid,de->fie", operator, covariance, precision=lax.Precision.HIGH)
    spectral_gram = jnp.einsum("fie,fje->fij", half, operator, precision=lax.Precision.HIGH)
    spectral_gram = spectral_gram / total_pixels
    return (spectral_gram, leading_mode(spectral_gram))


def solution(mesh):
    placed = (P("tm", ("group", "pix", "sub")), P(), P())
    return jax.shard_map(
        shards,
        mesh=mesh,
        in_specs=placed,
        out_specs=(P(("group", "tm"), None, None), P(("group", "tm"))),
        check_vma=False,
    )
```

```python
import functools
import math

import jax
import jax.numpy as jnp
from jax import lax
from jax.experimental import pallas as pl
from jax.experimental.pallas import tpu as pltpu
from jax.sharding import PartitionSpec as P

NFFT = 256
NB = 32
POWER = 8
NF = 128


power_eps = 1e-06


CHUNKS = 4


def windows_of(taper, step, length):
    steps = step.astype(jnp.float32)
    phase = steps * (2.0 * math.pi / length)
    center = (steps + 0.5) * (math.pi / length)
    sine_win = jnp.sin(center)
    hann = sine_win * sine_win
    hamming = 0.54 - 0.46 * jnp.cos(phase)
    blackman = 0.42 - 0.5 * jnp.cos(phase) + 0.08 * jnp.cos(2.0 * phase)
    chosen = jnp.where(
        taper == 0, hann, jnp.where(taper == 1, hamming, jnp.where(taper == 2, blackman, sine_win))
    )
    return jnp.where((step >= 0) & (step < length), chosen, 0.0)


def upright(row):
    square = (NB, NB)
    diagonal = lax.broadcasted_iota(jnp.int32, square, 0) == lax.broadcasted_iota(jnp.int32, square, 1)
    values = jnp.broadcast_to(row[...].astype(jnp.float32), square)
    return jnp.sum(jnp.where(diagonal, values, 0.0), axis=1, keepdims=True).astype(jnp.int32)


def split(value):
    high = value.astype(jnp.bfloat16)
    return high, (value - high.astype(jnp.float32)).astype(jnp.bfloat16)


def write_operator(offsets, taper, operator, operator_low):
    own, _, days = operator.shape
    step = lax.broadcasted_iota(jnp.int32, (NB, days), 1) - upright(offsets)
    windows = windows_of(jnp.broadcast_to(upright(taper), (NB, days)), step, NFFT)
    scaled = windows * (1.0 / jnp.sqrt(jnp.sum(windows * windows, axis=1, keepdims=True)))
    first = lax.axis_index("tm") * own

    def one(f, carry):
        angle = (((first + f) * step) & (NFFT - 1)).astype(jnp.float32) * (2.0 * math.pi / NFFT)
        for rows, table in ((pl.ds(0, NB), jnp.cos(angle)), (pl.ds(NB, NB), -jnp.sin(angle))):
            high, low = split(table.astype(jnp.bfloat16).astype(jnp.float32) * scaled)
            operator[f, rows, :] = high
            operator_low[f, rows, :] = low
        return carry

    lax.fori_loop(0, own, one, 0)


BLOCK = 128
MESH = pl.DeviceIdType.MESH


def stages_of(tm, pix, sub):
    if sub > 1 or tm % 2:
        split = [("sub", 1, sub), ("pix", 1, pix), ("tm", 1, tm)]
    else:
        split = [("tm", 1, 2), ("pix", 1, pix), ("tm", 2, tm // 2)]
    return split


def place_in(stage):
    axis, inner, members = stage
    return lax.rem(lax.axis_index(axis) // inner, members)


def device_at(stage, shift):
    axis, inner, members = stage
    index = lax.axis_index(axis)
    here = place_in(stage)
    there = lax.rem(here + shift, members)
    return {axis: index + (there - here) * inner}, there


def add_products(series, packed, first):
    blocks = series.shape[0] // BLOCK
    place = 0
    for i in range(blocks):
        strip = lax.dot_general(
            series[i * BLOCK : (i + 1) * BLOCK, :],
            series[i * BLOCK :, :],
            (((1,), (1,)), ((), ())),
            preferred_element_type=jnp.float32,
        )
        for j in range(blocks - i):
            rows = pl.ds((place + j) * BLOCK, BLOCK)
            block = strip[:, j * BLOCK : (j + 1) * BLOCK]
            packed[rows, :] = block if first else packed[rows, :] + block
        place += blocks - i


def covariance_kernel(
    stages, anomaly, offsets, taper, out, operator, operator_low, series, packed, gathered, own_sem, *scratch
):
    exchange_send, exchange_recv = scratch[:2]
    landing, sems = scratch[2:5], scratch[5:]
    chunks, days, width = series.shape
    per_device = anomaly.shape[0]
    peers = days // per_device
    me = lax.axis_index("tm")

    barrier = pltpu.get_barrier_semaphore()
    greeted = 0
    for axis in ("tm", "pix", "sub"):
        members = lax.axis_size(axis)
        for shift in range(1, members):
            device = {axis: lax.rem(lax.axis_index(axis) + shift, members)}
            pl.semaphore_signal(barrier, inc=1, device_id=device, device_id_type=MESH)
            greeted += 1
    my_rows = pl.ds(pl.multiple_of(me * per_device, per_device), per_device)

    def columns(device, chunk):
        return pl.ds(pl.multiple_of(device * (chunks * width) + chunk * width, width), width)

    kept = []
    for chunk in range(chunks):
        copy = pltpu.make_async_copy(
            anomaly.at[:, columns(me, chunk)], series.at[chunk, my_rows, :], own_sem.at[chunk]
        )
        copy.start()
        kept.append(copy)
    pl.semaphore_wait(barrier, greeted)
    farthest_first = sorted(range(1, peers), key=lambda shift: abs(2 * shift - peers))
    exchanged = []
    for chunk in range(chunks):
        copies = []
        for shift in farthest_first:
            there = lax.rem(me + shift, peers)
            copy = pltpu.make_async_remote_copy(
                src_ref=anomaly.at[:, columns(there, chunk)],
                dst_ref=series.at[chunk, my_rows, :],
                send_sem=exchange_send.at[chunk, shift - 1],
                recv_sem=exchange_recv.at[chunk, shift - 1],
                device_id={"tm": there},
                device_id_type=MESH,
            )
            copy.start()
            copies.append(copy)
        exchanged.append(copies)

    write_operator(offsets, taper, operator, operator_low)
    blocks = days // BLOCK
    filled = blocks * (blocks + 1) // 2 * BLOCK
    if packed.shape[0] > filled:
        packed[filled:, :] = jnp.zeros((packed.shape[0] - filled, BLOCK), jnp.float32)
    for chunk in range(chunks):
        kept[chunk].wait()
        for copy in exchanged[chunk]:
            copy.wait()
        add_products(series.at[chunk], packed, chunk == 0)

    near, side, line = stages
    piece = packed.shape[0] // line[2]
    half = piece // near[2]
    part = half // side[2]

    def rows_of(at, n, s, rows):
        return pl.ds(pl.multiple_of(at * piece + n * half + s * part, 8), rows)

    def send(src, dst, sem, index, device):
        copy = pltpu.make_async_remote_copy(
            src_ref=src,
            dst_ref=dst,
            send_sem=sems[2 * sem].at[index],
            recv_sem=sems[2 * sem + 1].at[index],
            device_id=device,
            device_id_type=MESH,
        )
        copy.start()
        return copy

    my_near, my_side = place_in(near), place_in(side)
    order = list(range(1, line[2])) + [0]
    order.sort(key=lambda shift: abs(2 * shift - line[2]))
    targets = {shift: device_at(line, shift) for shift in order}

    near_copies, side_copies, line_copies = {}, {}, {}
    for shift in order:
        at = targets[shift][1]
        near_copies[shift] = []
        for k in range(1, near[2]):
            device, there = device_at(near, k)
            index = shift * (near[2] - 1) + k - 1
            src = packed.at[rows_of(at, there, 0, half), :]
            near_copies[shift].append(send(src, landing[0].at[index], 0, index, device))
    for shift in order:
        at = targets[shift][1]
        mine = packed.at[rows_of(at, my_near, 0, half), :]
        total = mine[...]
        for k, copy in enumerate(near_copies[shift]):
            copy.wait()
            total = total + landing[0][shift * (near[2] - 1) + k]
        mine[...] = total
        side_copies[shift] = []
        for k in range(1, side[2]):
            device, there = device_at(side, k)
            index = shift * (side[2] - 1) + k - 1
            src = packed.at[rows_of(at, my_near, there, part), :]
            side_copies[shift].append(send(src, landing[1].at[index], 1, index, device))
    for shift in order:
        device, at = targets[shift]
        mine = packed.at[rows_of(at, my_near, my_side, part), :]
        total = mine[...]
        for k, copy in enumerate(side_copies[shift]):
            copy.wait()
            total = total + landing[1][shift * (side[2] - 1) + k]
        mine[...] = total
        if shift:
            line_copies[shift] = send(mine, landing[2].at[shift - 1], 2, shift - 1, device)
    here = place_in(line)
    own = gathered.at[rows_of(here, my_near, my_side, part), :]
    total = packed[rows_of(here, my_near, my_side, part), :]
    for shift in order:
        if shift:
            line_copies[shift].wait()
            total = total + landing[2][shift - 1]
    own[...] = total

    arriving = {}
    for shift in order:
        if shift:
            arriving[shift] = send(own, own, 3, shift - 1, targets[shift][0])
    spread, near_spread = {}, []
    incoming = [0] + [shift for shift in order if shift]
    sources = {shift: lax.rem(here + line[2] - shift, line[2]) for shift in incoming}
    for shift in incoming:
        if shift:
            arriving[shift].wait()
        mine = gathered.at[rows_of(sources[shift], my_near, my_side, part), :]
        spread[shift] = [
            send(mine, mine, 4, shift * (side[2] - 1) + k - 1, device_at(side, k)[0])
            for k in range(1, side[2])
        ]
    for shift in incoming:
        for copy in spread[shift]:
            copy.wait()
        mine = gathered.at[rows_of(sources[shift], my_near, 0, half), :]
        near_spread += [
            send(mine, mine, 5, shift * (near[2] - 1) + k - 1, device_at(near, k)[0])
            for k in range(1, near[2])
        ]
    for copy in near_spread:
        copy.wait()

    place = 0
    for i in range(blocks):
        for j in range(i, blocks):
            block = gathered[pl.ds(place * BLOCK, BLOCK), :]
            out[pl.ds(i * BLOCK, BLOCK), pl.ds(j * BLOCK, BLOCK)] = block
            if j > i:
                out[pl.ds(j * BLOCK, BLOCK), pl.ds(i * BLOCK, BLOCK)] = block.T
            place += 1


def covariance_and_operator(anomaly, offsets, taper_index):
    per_device, pixels = anomaly.shape
    peers = lax.axis_size("tm")
    days = per_device * peers
    own = NF // peers
    stages = stages_of(peers, lax.axis_size("pix"), lax.axis_size("sub"))
    devices = math.prod(stage[2] for stage in stages)
    blocks = days // BLOCK
    rows = -(-(blocks * (blocks + 1) // 2 * BLOCK) // (8 * devices)) * 8 * devices
    near, side, line = (stage[2] for stage in stages)
    half = rows // line // near
    part = half // side
    slots = [max(1, count) for count in (line * (near - 1), line * (side - 1), line - 1)]
    landing = [
        pltpu.VMEM((count, depth, BLOCK), jnp.float32)
        for count, depth in zip(slots, (half, part, part))
    ]
    sems = [
        pltpu.SemaphoreType.DMA((slots[stage],)) for stage in (0, 1, 2, 2, 1, 0) for _ in range(2)
    ]
    words = rows * BLOCK * 2 + days * days + own * 2 * NB * days + days * (pixels // peers) // 2
    words += sum(count * depth * BLOCK for count, depth in zip(slots, (half, part, part)))
    vmem = pl.BlockSpec(memory_space=pltpu.VMEM)
    return pl.pallas_call(
        functools.partial(covariance_kernel, stages),
        out_shape=(
            jax.ShapeDtypeStruct((days, days), jnp.float32),
            jax.ShapeDtypeStruct((own, 2 * NB, days), jnp.bfloat16),
            jax.ShapeDtypeStruct((own, 2 * NB, days), jnp.bfloat16),
        ),
        in_specs=[pl.BlockSpec(memory_space=pltpu.HBM), vmem, vmem],
        out_specs=(vmem, vmem, vmem),
        scratch_shapes=[
            pltpu.VMEM((CHUNKS, days, pixels // peers // CHUNKS), jnp.bfloat16),
            pltpu.VMEM((rows, BLOCK), jnp.float32),
            pltpu.VMEM((rows, BLOCK), jnp.float32),
            pltpu.SemaphoreType.DMA((CHUNKS,)),
            pltpu.SemaphoreType.DMA((CHUNKS, peers - 1)),
            pltpu.SemaphoreType.DMA((CHUNKS, peers - 1)),
        ]
        + landing
        + sems,
        compiler_params=pltpu.CompilerParams(
            collective_id=0, has_side_effects=True, vmem_limit_bytes=4 * words + 8 * 2**20
        ),
        name="covariance",
    )(anomaly, offsets[None, :], taper_index[None, :])


def finish_kernel(pixels, covariance, operator, operator_low, gram, lead, high, low):
    own, size, days = operator.shape
    high[...], low[...] = split(covariance[...])
    group = math.gcd(own, 4)

    def product(left, right, contract):
        return lax.dot_general(
            left, right, (((1,), (contract,)), ((), ())), preferred_element_type=jnp.float32
        )

    for first in range(0, own, group):
        left = operator[first : first + group].reshape(group * size, days)
        left_low = operator_low[first : first + group].reshape(group * size, days)
        half = product(left, high[...], 0) + (
            product(left_low, high[...], 0) + product(left, low[...], 0)
        )
        half_high, half_low = split(half)
        for f in range(group):
            rows = slice(f * size, (f + 1) * size)
            right, right_low = operator[first + f], operator_low[first + f]
            value = product(half_high[rows], right, 1) + (
                product(half_low[rows], right, 1) + product(half_high[rows], right_low, 1)
            )
            gram[first + f] = value / pixels

    matrix = gram[...]
    vector = jnp.ones((own, 1, size), jnp.float32)
    for step in range(POWER + 1):
        across = 2 - step % 2
        applied = jnp.sum(matrix * vector, axis=across, keepdims=True)
        power = jnp.sum(applied * applied, axis=3 - across, keepdims=True) / size
        vector = applied / jnp.sqrt(power + power_eps)
    column = jnp.broadcast_to(jnp.sqrt(power)[:, 0, :], (own, own))
    square = (own, own)
    diagonal = lax.broadcasted_iota(jnp.int32, square, 0) == lax.broadcasted_iota(jnp.int32, square, 1)
    lead[...] = jnp.sum(jnp.where(diagonal, column, 0.0), axis=0, keepdims=True)


def gram_and_leading(covariance, operator, operator_low, pixels):
    own, size, days = operator.shape
    vmem = pl.BlockSpec(memory_space=pltpu.VMEM)
    gram, lead = pl.pallas_call(
        functools.partial(finish_kernel, pixels),
        out_shape=(
            jax.ShapeDtypeStruct((own, size, size), jnp.float32),
            jax.ShapeDtypeStruct((1, own), jnp.float32),
        ),
        in_specs=[vmem] * 3,
        out_specs=(vmem, vmem),
        scratch_shapes=[pltpu.VMEM((days, days), jnp.bfloat16)] * 2,
        compiler_params=pltpu.CompilerParams(
            vmem_limit_bytes=8 * days * days + 4 * own * size * days + 12 * 2**20
        ),
        name="finish",
    )(covariance, operator, operator_low)
    return gram, lead[0]


def shards(anomaly, offsets, taper_index):
    total_pixels = anomaly.shape[1] * lax.axis_size(("pix", "sub"))
    covariance, operator, operator_low = covariance_and_operator(anomaly, offsets, taper_index)
    return gram_and_leading(covariance, operator, operator_low, total_pixels)


def solution(mesh):
    placed = (P("tm", ("group", "pix", "sub")), P(), P())
    return jax.shard_map(
        shards,
        mesh=mesh,
        in_specs=placed,
        out_specs=(P(("group", "tm"), None, None), P(("group", "tm"))),
        check_vma=False,
    )
```

```python
import functools
import math

import jax
import jax.numpy as jnp
from jax import lax
from jax.experimental import pallas as pl
from jax.experimental.pallas import tpu as pltpu
from jax.sharding import PartitionSpec as P

NFFT = 256
NB = 32
POWER = 8
NF = 128


power_eps = 1e-06


CHUNKS = 4


def windows_of(taper, step, length):
    steps = step.astype(jnp.float32)
    phase = steps * (2.0 * math.pi / length)
    center = (steps + 0.5) * (math.pi / length)
    sine_win = jnp.sin(center)
    hann = sine_win * sine_win
    hamming = 0.54 - 0.46 * jnp.cos(phase)
    blackman = 0.42 - 0.5 * jnp.cos(phase) + 0.08 * jnp.cos(2.0 * phase)
    chosen = jnp.where(
        taper == 0, hann, jnp.where(taper == 1, hamming, jnp.where(taper == 2, blackman, sine_win))
    )
    return jnp.where((step >= 0) & (step < length), chosen, 0.0)


def upright(row):
    square = (NB, NB)
    diagonal = lax.broadcasted_iota(jnp.int32, square, 0) == lax.broadcasted_iota(jnp.int32, square, 1)
    values = jnp.broadcast_to(row[...].astype(jnp.float32), square)
    return jnp.sum(jnp.where(diagonal, values, 0.0), axis=1, keepdims=True).astype(jnp.int32)


def split(value):
    high = value.astype(jnp.bfloat16)
    return high, (value - high.astype(jnp.float32)).astype(jnp.bfloat16)


def write_operator(offsets, taper, operator, operator_low):
    own, _, days = operator.shape
    step = lax.broadcasted_iota(jnp.int32, (NB, days), 1) - upright(offsets)
    windows = windows_of(jnp.broadcast_to(upright(taper), (NB, days)), step, NFFT)
    scaled = windows * (1.0 / jnp.sqrt(jnp.sum(windows * windows, axis=1, keepdims=True)))
    first = lax.axis_index("tm") * own

    def one(f, carry):
        angle = (((first + f) * step) & (NFFT - 1)).astype(jnp.float32) * (2.0 * math.pi / NFFT)
        for rows, table in ((pl.ds(0, NB), jnp.cos(angle)), (pl.ds(NB, NB), -jnp.sin(angle))):
            high, low = split(table.astype(jnp.bfloat16).astype(jnp.float32) * scaled)
            operator[f, rows, :] = high
            operator_low[f, rows, :] = low
        return carry

    lax.fori_loop(0, own, one, 0)


BLOCK = 128
MESH = pl.DeviceIdType.MESH


def stages_of(tm, pix, sub):
    if sub > 1 or tm % 2:
        split = [("sub", 1, sub), ("pix", 1, pix), ("tm", 1, tm)]
    else:
        split = [("tm", 1, 2), ("pix", 1, pix), ("tm", 2, tm // 2)]
    return split


def place_in(stage):
    axis, inner, members = stage
    return lax.rem(lax.axis_index(axis) // inner, members)


def device_at(stage, shift):
    axis, inner, members = stage
    index = lax.axis_index(axis)
    here = place_in(stage)
    there = lax.rem(here + shift, members)
    return {axis: index + (there - here) * inner}, there


def finish(pixels, high, low, operator, operator_low, gram, lead):
    own, size, days = operator.shape
    group = math.gcd(own, 4)

    def product(left, right, contract):
        return lax.dot_general(
            left, right, (((1,), (contract,)), ((), ())), preferred_element_type=jnp.float32
        )

    for first in range(0, own, group):
        left = operator[first : first + group].reshape(group * size, days)
        left_low = operator_low[first : first + group].reshape(group * size, days)
        half = product(left, high[...], 0) + (
            product(left_low, high[...], 0) + product(left, low[...], 0)
        )
        half_high, half_low = split(half)
        for f in range(group):
            rows = slice(f * size, (f + 1) * size)
            right, right_low = operator[first + f], operator_low[first + f]
            value = product(half_high[rows], right, 1) + (
                product(half_low[rows], right, 1) + product(half_high[rows], right_low, 1)
            )
            gram[first + f] = value / pixels

    matrix = gram[...]
    vector = jnp.ones((own, 1, size), jnp.float32)
    for step in range(POWER + 1):
        across = 2 - step % 2
        applied = jnp.sum(matrix * vector, axis=across, keepdims=True)
        power = jnp.sum(applied * applied, axis=3 - across, keepdims=True) / size
        vector = applied / jnp.sqrt(power + power_eps)
    column = jnp.broadcast_to(jnp.sqrt(power)[:, 0, :], (own, own))
    square = (own, own)
    diagonal = lax.broadcasted_iota(jnp.int32, square, 0) == lax.broadcasted_iota(jnp.int32, square, 1)
    lead[...] = jnp.sum(jnp.where(diagonal, column, 0.0), axis=0, keepdims=True)


def add_products(series, packed, first):
    blocks = series.shape[0] // BLOCK
    place = 0
    for i in range(blocks):
        strip = lax.dot_general(
            series[i * BLOCK : (i + 1) * BLOCK, :],
            series[i * BLOCK :, :],
            (((1,), (1,)), ((), ())),
            preferred_element_type=jnp.float32,
        )
        for j in range(blocks - i):
            rows = pl.ds((place + j) * BLOCK, BLOCK)
            block = strip[:, j * BLOCK : (j + 1) * BLOCK]
            packed[rows, :] = block if first else packed[rows, :] + block
        place += blocks - i


def covariance_kernel(
    stages,
    pixels,
    anomaly,
    offsets,
    taper,
    gram,
    lead,
    high,
    low,
    operator,
    operator_low,
    series,
    packed,
    gathered,
    own_sem,
    *scratch,
):
    exchange_send, exchange_recv = scratch[:2]
    landing, sems = scratch[2:5], scratch[5:]
    chunks, days, width = series.shape
    per_device = anomaly.shape[0]
    peers = days // per_device
    me = lax.axis_index("tm")

    barrier = pltpu.get_barrier_semaphore()
    greeted = 0
    for axis in ("tm", "pix", "sub"):
        members = lax.axis_size(axis)
        for shift in range(1, members):
            device = {axis: lax.rem(lax.axis_index(axis) + shift, members)}
            pl.semaphore_signal(barrier, inc=1, device_id=device, device_id_type=MESH)
            greeted += 1
    my_rows = pl.ds(pl.multiple_of(me * per_device, per_device), per_device)

    def columns(device, chunk):
        return pl.ds(pl.multiple_of(device * (chunks * width) + chunk * width, width), width)

    kept = []
    for chunk in range(chunks):
        copy = pltpu.make_async_copy(
            anomaly.at[:, columns(me, chunk)], series.at[chunk, my_rows, :], own_sem.at[chunk]
        )
        copy.start()
        kept.append(copy)
    pl.semaphore_wait(barrier, greeted)
    farthest_first = sorted(range(1, peers), key=lambda shift: abs(2 * shift - peers))
    exchanged = []
    for chunk in range(chunks):
        copies = []
        for shift in farthest_first:
            there = lax.rem(me + shift, peers)
            copy = pltpu.make_async_remote_copy(
                src_ref=anomaly.at[:, columns(there, chunk)],
                dst_ref=series.at[chunk, my_rows, :],
                send_sem=exchange_send.at[chunk, shift - 1],
                recv_sem=exchange_recv.at[chunk, shift - 1],
                device_id={"tm": there},
                device_id_type=MESH,
            )
            copy.start()
            copies.append(copy)
        exchanged.append(copies)

    write_operator(offsets, taper, operator, operator_low)
    blocks = days // BLOCK
    filled = blocks * (blocks + 1) // 2 * BLOCK
    if packed.shape[0] > filled:
        packed[filled:, :] = jnp.zeros((packed.shape[0] - filled, BLOCK), jnp.float32)
    for chunk in range(chunks):
        kept[chunk].wait()
        for copy in exchanged[chunk]:
            copy.wait()
        add_products(series.at[chunk], packed, chunk == 0)

    near, side, line = stages
    piece = packed.shape[0] // line[2]
    half = piece // near[2]
    part = half // side[2]

    def rows_of(at, n, s, rows):
        return pl.ds(pl.multiple_of(at * piece + n * half + s * part, 8), rows)

    def send(src, dst, sem, index, device):
        copy = pltpu.make_async_remote_copy(
            src_ref=src,
            dst_ref=dst,
            send_sem=sems[2 * sem].at[index],
            recv_sem=sems[2 * sem + 1].at[index],
            device_id=device,
            device_id_type=MESH,
        )
        copy.start()
        return copy

    my_near, my_side = place_in(near), place_in(side)
    order = list(range(1, line[2])) + [0]
    order.sort(key=lambda shift: abs(2 * shift - line[2]))
    targets = {shift: device_at(line, shift) for shift in order}

    near_copies, side_copies, line_copies = {}, {}, {}
    for shift in order:
        at = targets[shift][1]
        near_copies[shift] = []
        for k in range(1, near[2]):
            device, there = device_at(near, k)
            index = shift * (near[2] - 1) + k - 1
            src = packed.at[rows_of(at, there, 0, half), :]
            near_copies[shift].append(send(src, landing[0].at[index], 0, index, device))
    for shift in order:
        at = targets[shift][1]
        mine = packed.at[rows_of(at, my_near, 0, half), :]
        total = mine[...]
        for k, copy in enumerate(near_copies[shift]):
            copy.wait()
            total = total + landing[0][shift * (near[2] - 1) + k]
        mine[...] = total
        side_copies[shift] = []
        for k in range(1, side[2]):
            device, there = device_at(side, k)
            index = shift * (side[2] - 1) + k - 1
            src = packed.at[rows_of(at, my_near, there, part), :]
            side_copies[shift].append(send(src, landing[1].at[index], 1, index, device))
    for shift in order:
        device, at = targets[shift]
        mine = packed.at[rows_of(at, my_near, my_side, part), :]
        total = mine[...]
        for k, copy in enumerate(side_copies[shift]):
            copy.wait()
            total = total + landing[1][shift * (side[2] - 1) + k]
        mine[...] = total
        if shift:
            line_copies[shift] = send(mine, landing[2].at[shift - 1], 2, shift - 1, device)
    here = place_in(line)
    own = gathered.at[rows_of(here, my_near, my_side, part), :]
    total = packed[rows_of(here, my_near, my_side, part), :]
    for shift in order:
        if shift:
            line_copies[shift].wait()
            total = total + landing[2][shift - 1]
    own[...] = total

    arriving = {}
    for shift in order:
        if shift:
            arriving[shift] = send(own, own, 3, shift - 1, targets[shift][0])
    spread, near_spread = {}, []
    incoming = [0] + [shift for shift in order if shift]
    sources = {shift: lax.rem(here + line[2] - shift, line[2]) for shift in incoming}
    for shift in incoming:
        if shift:
            arriving[shift].wait()
        mine = gathered.at[rows_of(sources[shift], my_near, my_side, part), :]
        spread[shift] = [
            send(mine, mine, 4, shift * (side[2] - 1) + k - 1, device_at(side, k)[0])
            for k in range(1, side[2])
        ]
    for shift in incoming:
        for copy in spread[shift]:
            copy.wait()
        mine = gathered.at[rows_of(sources[shift], my_near, 0, half), :]
        near_spread += [
            send(mine, mine, 5, shift * (near[2] - 1) + k - 1, device_at(near, k)[0])
            for k in range(1, near[2])
        ]
    for copy in near_spread:
        copy.wait()

    place = 0
    for i in range(blocks):
        for j in range(i, blocks):
            block = gathered[pl.ds(place * BLOCK, BLOCK), :]
            upper, lower = pl.ds(i * BLOCK, BLOCK), pl.ds(j * BLOCK, BLOCK)
            high[upper, lower], low[upper, lower] = split(block)
            if j > i:
                high[lower, upper], low[lower, upper] = split(block.T)
            place += 1
    finish(pixels, high, low, operator, operator_low, gram, lead)


def gram_and_leading(anomaly, offsets, taper_index):
    per_device, pixels = anomaly.shape
    peers = lax.axis_size("tm")
    days = per_device * peers
    own = NF // peers
    total_pixels = pixels * lax.axis_size(("pix", "sub"))
    stages = stages_of(peers, lax.axis_size("pix"), lax.axis_size("sub"))
    devices = math.prod(stage[2] for stage in stages)
    blocks = days // BLOCK
    rows = -(-(blocks * (blocks + 1) // 2 * BLOCK) // (8 * devices)) * 8 * devices
    near, side, line = (stage[2] for stage in stages)
    half = rows // line // near
    part = half // side
    slots = [max(1, count) for count in (line * (near - 1), line * (side - 1), line - 1)]
    landing = [
        pltpu.VMEM((count, depth, BLOCK), jnp.float32)
        for count, depth in zip(slots, (half, part, part))
    ]
    sems = [
        pltpu.SemaphoreType.DMA((slots[stage],)) for stage in (0, 1, 2, 2, 1, 0) for _ in range(2)
    ]
    vmem = pl.BlockSpec(memory_space=pltpu.VMEM)
    return pl.pallas_call(
        functools.partial(covariance_kernel, stages, total_pixels),
        out_shape=(
            jax.ShapeDtypeStruct((own, 2 * NB, 2 * NB), jnp.float32),
            jax.ShapeDtypeStruct((1, own), jnp.float32),
        ),
        in_specs=[pl.BlockSpec(memory_space=pl.ANY), vmem, vmem],
        out_specs=(vmem, vmem),
        scratch_shapes=[pltpu.VMEM((days, days), jnp.bfloat16)] * 2
        + [pltpu.VMEM((own, 2 * NB, days), jnp.bfloat16)] * 2
        + [
            pltpu.VMEM((CHUNKS, days, pixels // peers // CHUNKS), jnp.bfloat16),
            pltpu.VMEM((rows, BLOCK), jnp.float32),
            pltpu.VMEM((rows, BLOCK), jnp.float32),
            pltpu.SemaphoreType.DMA((CHUNKS,)),
            pltpu.SemaphoreType.DMA((CHUNKS, peers - 1)),
            pltpu.SemaphoreType.DMA((CHUNKS, peers - 1)),
        ]
        + landing
        + sems,
        compiler_params=pltpu.CompilerParams(
            collective_id=0, has_side_effects=True, vmem_limit_bytes=58 * 2**20
        ),
        name="covariance",
    )(anomaly, offsets[None, :], taper_index[None, :])


def shards(anomaly, offsets, taper_index):
    gram, lead = gram_and_leading(anomaly, offsets, taper_index)
    return (gram, lead[0])


def solution(mesh):
    placed = (P("tm", ("group", "pix", "sub")), P(), P())
    return jax.shard_map(
        shards,
        mesh=mesh,
        in_specs=placed,
        out_specs=(P(("group", "tm"), None, None), P(("group", "tm"))),
        check_vma=False,
    )
```
